32 devices in a mesh: row: 4 (over x, core), col: 8 (over z, y).
Axes of the slice: x: 2, y: 2, z: 4, core: 2. Of those that a mesh axis runs over, the one named last changes fastest.
Arguments:
- near: float32 [8, 16, 3, 3, 256, 256], P('row', 'col'), may hold values from -0.01 to 3.7
- interp: float32 [8, 16, 160, 160], P('row', 'col'), may hold values from -0.5 to 0.5
- red_count: int32 [8, 16], P('row', 'col'), may hold values from 96 to 160
- owner_flip: int32 [4, 8, 2], P('row', 'col'), may hold values from 0 to 1, as said below
Outputs:
- parents: float32 [4, 8, 640, 640], P('row', 'col')
The draws below stay inside these ranges and needn't reach their ends.
Inputs may be any that keep to these rules, and one draw needn't show every extreme that they name: owner_flip[i, j, :] is the same on the four devices of each aligned 2 x 2 group, rows 2 i and 2 i + 1, columns 2 j and 2 j + 1.
All inputs are finite; a program needn't handle non-finite values.
Results may differ from the reference program's by a relative error of at most 0.0001.
Values sent between devices are 32-bit elements; how exact they have to be, the bound alone decides.
A program may use at most 128 MiB of HBM per device.

```python
import math
import jax
import jax.numpy as jnp
from jax import lax

PTS = 256
SLOTS = 160
LOW = 96
BR = 8
BC = 16
N_ROW = 4
N_COL = 8


FORWARD = ((0, 1), (1, -1), (1, 0), (1, 1))


def draw_near(key, part):
    offsets = jax.random.uniform(jax.random.fold_in(key, 101), (BR, BC, 2, PTS), jnp.float32)
    coefficient = jnp.exp(jax.random.uniform(jax.random.fold_in(key, 102), (BR, BC, PTS), jnp.float32, math.log(0.2), math.log(0.6)))
    diag_values = jax.random.uniform(jax.random.fold_in(key, 103), (BR, BC, PTS), jnp.float32, 1.0, 2.0)
    row_places = jnp.arange(BR, dtype=jnp.int32).astype(jnp.float32)
    col_places = jnp.arange(BC, dtype=jnp.int32).astype(jnp.float32)
    pos_x = row_places[:, None, None] + offsets[:, :, 0, :]
    pos_y = col_places[None, :, None] + offsets[:, :, 1, :]
    pad_x = jnp.pad(pos_x, ((1, 1), (1, 1), (0, 0)))
    pad_y = jnp.pad(pos_y, ((1, 1), (1, 1), (0, 0)))
    pad_coef = jnp.pad(coefficient, ((1, 1), (1, 1), (0, 0)))
    identity = jnp.eye(PTS, dtype=jnp.float32)
    store = jnp.zeros((BR, BC, 3, 3, PTS, PTS), jnp.float32)
    for row_step in (-1, 0, 1):
        for col_step in (-1, 0, 1):
            other_x = pad_x[1 + row_step:1 + row_step + BR, 1 + col_step:1 + col_step + BC]
            other_y = pad_y[1 + row_step:1 + row_step + BR, 1 + col_step:1 + col_step + BC]
            other_coef = pad_coef[1 + row_step:1 + row_step + BR, 1 + col_step:1 + col_step + BC]
            delta_x = pos_x[:, :, :, None] - other_x[:, :, None, :]
            delta_y = pos_y[:, :, :, None] - other_y[:, :, None, :]
            distance = jnp.sqrt(delta_x * delta_x + delta_y * delta_y)
            block = coefficient[:, :, :, None] * other_coef[:, :, None, :] * jnp.exp(-distance / 0.5)
            if row_step == 0 and col_step == 0:
                block = block + identity * diag_values[:, :, :, None]
            store = store.at[:, :, row_step + 1, col_step + 1].set(block)
    valid = jnp.pad(jnp.ones((BR, BC), jnp.float32), ((1, 1), (1, 1)))
    for number, (row_step, col_step) in enumerate(FORWARD):
        rough = jax.random.uniform(jax.random.fold_in(key, 110 + number), (BR, BC, PTS, PTS), jnp.float32, -0.01, 0.01)
        valid_here = valid[1 + row_step:1 + row_step + BR, 1 + col_step:1 + col_step + BC]
        rough = rough * valid_here[:, :, None, None]
        store = store.at[:, :, 1 + row_step, 1 + col_step].add(rough)
        padded_rough = jnp.pad(rough, ((1, 1), (1, 1), (0, 0), (0, 0)))
        behind = padded_rough[1 - row_step:1 - row_step + BR, 1 - col_step:1 - col_step + BC]
        store = store.at[:, :, 1 - row_step, 1 - col_step].add(jnp.swapaxes(behind, 2, 3))
    rough_centre = jax.random.uniform(jax.random.fold_in(key, 120), (BR, BC, PTS, PTS), jnp.float32, -0.01, 0.01)
    store = store.at[:, :, 1, 1].add(0.5 * (rough_centre + jnp.swapaxes(rough_centre, 2, 3)))
    return store


def draw_red_count(key, part):
    base_counts = jax.random.randint(jax.random.fold_in(key, 201), (BR * BC,), PTS - SLOTS, SLOTS + 1)
    shuffled = jax.random.permutation(jax.random.fold_in(key, 202), BR * BC)
    base_counts = base_counts.at[shuffled[0]].set(PTS - SLOTS)
    base_counts = base_counts.at[shuffled[1]].set(SLOTS)
    return base_counts.reshape(BR, BC).astype(jnp.int32)


def draw_owner_flip(key, part):
    groups = jax.random.randint(jax.random.fold_in(key, 301), (BR // 4 * (BC // 4), 2), 0, 2)
    groups = groups.at[0].set(jnp.array([0, 1], dtype=jnp.int32))
    groups = groups.at[1].set(jnp.array([1, 0], dtype=jnp.int32))
    groups = groups.reshape(BR // 4, BC // 4, 2)
    spread = jnp.repeat(jnp.repeat(groups, 2, axis=0), 2, axis=1)
    return spread.astype(jnp.int32)


def block_scale(key, shape, pieces, low, high):
    def one(axis_at, shards_of):
        draws = jax.random.uniform(jax.random.fold_in(jax.random.fold_in(key, 6), axis_at), (shards_of,), jnp.float32, low / len(pieces), high / len(pieces))
        return jnp.repeat(jnp.exp(draws), shape[axis_at] // shards_of).reshape((-1,) + (1,) * (len(shape) - axis_at - 1))

    loudness = one(*pieces[0])
    for cut in pieces[1:]:
        loudness = loudness * one(*cut)
    return loudness


def normal_values(stream_key, dims, width, most, pieces=(), kind=jnp.bfloat16):
    values = width * jax.random.normal(stream_key, dims, jnp.float32)
    if pieces:
        values = values * block_scale(stream_key, dims, pieces, -0.22, 0.18)
    return jnp.clip(values, -most, most).astype(kind)


def setup_inputs(seed: int = 0) -> dict:
    key_list = jax.random.split(jax.random.key(seed), 5)
    near = draw_near(jax.random.fold_in(key_list[4], 71), 0)
    interp = normal_values(key_list[1], (BR, BC, SLOTS, SLOTS), 0.08, 0.5, ((0, 4), (1, 8)), jnp.float32)
    red_count = draw_red_count(jax.random.fold_in(key_list[4], 71), 0)
    owner_flip = draw_owner_flip(jax.random.fold_in(key_list[4], 71), 0)
    return {"near": near, "interp": interp, "red_count": red_count, "owner_flip": owner_flip}


COLOURS = ((0, 0), (0, 1), (1, 0), (1, 1))
STEPS = (-1, 0, 1)
PRECISE = lax.Precision.HIGHEST

def reference(near, interp, red_count, owner_flip):
    store = jnp.pad(near, ((1, 1), (1, 1), (0, 0), (0, 0), (0, 0), (0, 0)))
    slot_index = jnp.arange(SLOTS, dtype=jnp.int32)
    point_index = jnp.arange(PTS, dtype=jnp.int32)
    identity = jnp.eye(SLOTS, dtype=jnp.float32)
    for colour, (home_row, home_col) in enumerate(COLOURS):
        blocks = store[1 + home_row:1 + home_row + BR:2, 1 + home_col:1 + home_col + BC:2]
        red_here = red_count[home_row::2, home_col::2]
        mask_red = (slot_index[None, None, :] < red_here[:, :, None]).astype(jnp.float32)
        mask_skel = (slot_index[None, None, :] + LOW >= red_here[:, :, None]).astype(jnp.float32)
        interp_masked = interp[home_row::2, home_col::2] * mask_red[:, :, :, None] * mask_skel[:, :, None, :]
        reduced = blocks[:, :, :, :, :SLOTS, :] - jnp.einsum('ijrs,ijabst->ijabrt', interp_masked, blocks[:, :, :, :, LOW:, :], precision=PRECISE)
        active_rows = []
        for row_step in STEPS:
            line_list = []
            for col_step in STEPS:
                if row_step == 0 and col_step == 0:
                    active_here = point_index[None, None, :] >= red_here[:, :, None]
                else:
                    active_here = jnp.ones((N_ROW, N_COL, PTS), dtype=bool)
                line_list.append(active_here.astype(jnp.float32))
            active_rows.append(jnp.stack(line_list, axis=2))
        active = jnp.stack(active_rows, axis=2)
        inner_rows = reduced * mask_red[:, :, None, None, :, None] * active[:, :, :, :, None, :]
        centre = reduced[:, :, 1, 1]
        red_block = centre[:, :, :, :SLOTS] - jnp.einsum('ijrt,ijqt->ijrq', centre[:, :, :, LOW:], interp_masked, precision=PRECISE)
        both_masks = mask_red[:, :, :, None] * mask_red[:, :, None, :]
        padded = jnp.where(both_masks > 0, red_block, identity)
        lower_factor = jnp.linalg.cholesky(padded)
        stacked = inner_rows.transpose(0, 1, 4, 2, 3, 5).reshape(N_ROW, N_COL, SLOTS, 9 * PTS)
        solved = jax.scipy.linalg.solve_triangular(lower_factor, stacked, lower=True)
        panels = solved.reshape(N_ROW, N_COL, SLOTS, 3, 3, PTS)
        for row_first in STEPS:
            for col_first in STEPS:
                row_low = max(row_first - 1, -1)
                row_high = min(row_first + 1, 1)
                col_low = max(col_first - 1, -1)
                col_high = min(col_first + 1, 1)
                single = panels[:, :, :, row_first + 1, col_first + 1, :]
                paired = panels[:, :, :, row_low + 1:row_high + 2, col_low + 1:col_high + 2, :]
                update = jnp.einsum('ijrc,ijrabd->ijabcd', single, paired, precision=PRECISE)
                target_row = 1 + home_row + row_first
                target_col = 1 + home_col + col_first
                store = store.at[target_row:target_row + BR:2, target_col:target_col + BC:2, row_low - row_first + 1:row_high - row_first + 2, col_low - col_first + 1:col_high - col_first + 2].add(-update)
    inner_store = store[1:1 + BR, 1:1 + BC]
    mask_child = (slot_index[None, None, :] + LOW >= red_count[:, :, None]).astype(jnp.float32)
    row_blocks = []
    for first_row, first_col in COLOURS:
        line_list = []
        for second_row, second_col in COLOURS:
            piece_block = inner_store[first_row::2, first_col::2, second_row - first_row + 1, second_col - first_col + 1, LOW:, LOW:]
            piece_block = piece_block * mask_child[first_row::2, first_col::2][:, :, :, None] * mask_child[second_row::2, second_col::2][:, :, None, :]
            line_list.append(piece_block)
        row_blocks.append(jnp.concatenate(line_list, axis=3))
    parent = jnp.concatenate(row_blocks, axis=2)
    device_rows = jnp.arange(N_ROW, dtype=jnp.int32)
    device_cols = jnp.arange(N_COL, dtype=jnp.int32)
    partner_rows = device_rows + 1 - 2 * (device_rows % 2)
    partner_cols = device_cols + 1 - 2 * (device_cols % 2)
    source_rows = jnp.where(owner_flip[:, :, 0] == 1, partner_rows[:, None], device_rows[:, None])
    source_cols = jnp.where(owner_flip[:, :, 1] == 1, partner_cols[None, :], device_cols[None, :])
    return parent[source_rows, source_cols]
```

```python
import functools

import jax
import jax.numpy as jnp
from jax import lax
from jax.experimental import pallas as pl
from jax.experimental.pallas import tpu as pltpu
from jax.sharding import PartitionSpec as P

EXACT = lax.Precision.HIGHEST
GROUP = 8
BLOCK = 32
MESH = pl.DeviceIdType.MESH
LOW_FIRST = (0, -1)

FULL = [(a, e) for a in (-1, 0, 1) for e in (-1, 0, 1)]
TRAVEL = {
    "l0": [(0, -1), (1, 0), (-1, 0), (-1, -1), (1, -1), (0, 0)],
    "u0": [(-1, 0), (-1, -1), (0, -1), (0, 0), (-1, 1), (0, 1)],
    "d0": [(0, -1), (-1, 0), (-1, -1), (0, 0)],
    "r1": [(1, 1), (-1, 1), (-1, 0), (1, 0), (0, 1), (0, 0)],
    "u1": [(-1, -1), (-1, 0), (-1, 1), (0, -1), (0, 0), (0, 1)],
    "d1": [(-1, 1), (-1, 0), (0, 1), (0, 0)],
    "l2": [(0, -1), (-1, 0), (0, 0), (1, 0), (1, -1), (-1, -1)],
    "v2": [(1, 0), (1, 1)],
    "d2": [(1, -1)],
    "r3": [(-1, 1), (0, 1), (1, 1)],
    "v3": [(1, -1), (1, 0)],
    "d3": [(1, 1)],
}
FIRST = {}
COUNT = 0
for _name, _panels in TRAVEL.items():
    FIRST[_name] = COUNT
    COUNT += len(_panels)


def slot(name, k):
    return FIRST[name] + TRAVEL[name].index(k)


def near_at(k):
    return (k[0] + 1) * 3 + k[1] + 1


def split(value):
    high = value.astype(jnp.bfloat16)
    low = (value - high.astype(jnp.float32)).astype(jnp.bfloat16)
    return high, low


def dot(left, right):
    return jnp.dot(left, right, preferred_element_type=jnp.float32)


def diagonal_inverse(block):
    size = block.shape[0]
    rows = lax.broadcasted_iota(jnp.int32, (size, size), 0)
    cols = lax.broadcasted_iota(jnp.int32, (size, size), 1)
    eye = (rows == cols).astype(jnp.float32)
    wide = jnp.concatenate([block, eye, jnp.zeros((size, 128 - 2 * size), jnp.float32)], axis=1)
    row_ids = lax.broadcasted_iota(jnp.int32, (size, 128), 0)
    scale = jnp.ones((size, 128), jnp.float32)
    for start in range(0, size, GROUP):
        columns = [
            jnp.broadcast_to(wide[:, start + q : start + q + 1], (size, 128)) for q in range(GROUP)
        ]
        for q in range(GROUP):
            at = start + q
            pivot = columns[q][at : at + 1, :]
            inverse = 1.0 / pivot
            below = jnp.where(row_ids > at, columns[q], 0.0)
            scale = jnp.where(row_ids == at, lax.rsqrt(pivot), scale)
            wide = wide - below * (wide[at : at + 1, :] * inverse)
            for p in range(q + 1, GROUP):
                columns[p] = columns[p] - below * (columns[p][at : at + 1, :] * inverse)
    return (wide * scale)[:, size : 2 * size]


def factor_inverse(matrix, hooks=()):
    size = matrix.shape[0]
    rows = lax.broadcasted_iota(jnp.int32, (size, size), 0)
    cols = lax.broadcasted_iota(jnp.int32, (size, size), 1)
    rest = matrix
    right = (rows == cols).astype(jnp.float32)
    done = []
    for start in range(0, size, BLOCK):
        inverse = diagonal_inverse(rest[:BLOCK, :BLOCK])
        top_right = jnp.dot(inverse, right[:BLOCK], precision=EXACT)
        done.append(top_right)
        if start + BLOCK < size:
            top = jnp.dot(inverse, rest[:BLOCK, BLOCK:], precision=EXACT)
            top_t = top.T
            rest = rest[BLOCK:, BLOCK:] - jnp.dot(top_t, top, precision=EXACT)
            right = right[BLOCK:] - jnp.dot(top_t, top_right, precision=EXACT)
        for at, hook in hooks:
            if at == start // BLOCK:
                hook()
    return jnp.concatenate(done, axis=0)


def kernel(sizes, near, interp_all, counts, out, store, interp, panels, stacks, arrived, shared,
           pulled, send_sem, recv_sem, load_sem):
    n_row, n_col = sizes
    points, slots = store.shape[-1], interp.shape[-1]
    low = points - slots
    row, col = lax.axis_index("row"), lax.axis_index("col")
    has = {
        "up": row > 0, "down": row < n_row - 1, "left": col > 0, "right": col < n_col - 1,
    }
    where_to = {
        "up": {"row": row - 1, "col": col}, "down": {"row": row + 1, "col": col},
        "left": {"row": row, "col": col - 1}, "right": {"row": row, "col": col + 1},
    }

    loads = [pltpu.make_async_copy(interp_all.at[i // 2, i % 2], interp.at[i], load_sem.at[4 + i])
             for i in range(4)]
    loads = [pltpu.make_async_copy(near.at[i], store.at[i], load_sem.at[i]) for i in range(4)] + loads
    pulls = {}
    for y in range(4):
        for x in range(y):
            for one, two in ((x, y), (y, x)):
                k = near_at((two // 2 - one // 2, two % 2 - one % 2))
                n = len(pulls)
                pulls[one, two] = n, pltpu.make_async_copy(
                    near.at[one, k, pl.ds(low, slots), :], pulled.at[n], load_sem.at[8 + n]
                )
    loads[0].start()
    loads[4].start()
    for i in (1, 5, 2, 6, 3, 7):
        loads[i].start()
    for _, copy in pulls.values():
        copy.start()

    barrier = pltpu.get_barrier_semaphore()
    for way in has:
        @pl.when(has[way])
        def _(way=way):
            pl.semaphore_signal(barrier, inc=1, device_id=where_to[way], device_id_type=MESH)

    sent = []

    def copy_of(name, k, source, way):
        i = slot(name, k)
        return pltpu.make_async_remote_copy(
            src_ref=source, dst_ref=arrived.at[i], send_sem=send_sem.at[i],
            recv_sem=recv_sem.at[i], device_id=where_to[way], device_id_type=MESH,
        )

    def send(name, k, source, way, and_also=None):
        copy = copy_of(name, k, source, way)
        sent.append((copy, way, and_also))
        if and_also is None:
            pl.when(has[way])(copy.start)
        else:
            pl.when(has[way] & has[and_also])(copy.start)

    def make_stack(value, ref):
        high, less = split(value)
        ref[0:slots] = high
        ref[slots : 2 * slots] = high
        ref[2 * slots : 3 * slots] = less
        ref[3 * slots : 4 * slots] = high

    def receive(name, k, stack):
        i = slot(name, k)
        pltpu.make_async_remote_copy(
            src_ref=arrived.at[i], dst_ref=arrived.at[i], send_sem=send_sem.at[i],
            recv_sem=recv_sem.at[i], device_id=where_to["up"], device_id_type=MESH,
        ).wait_recv()
        make_stack(arrived[i], stack.at[near_at(k)])

    def update(x, stack, one, twos):
        for two in twos:
            at = near_at((two[0] - one[0], two[1] - one[1]))
            store[x, at] = store[x, at] - lax.dot_general(
                stack[near_at(one), 0 : 3 * slots], stack[near_at(two), slots : 4 * slots],
                (((0,), (0,)), ((), ())), preferred_element_type=jnp.float32,
            )

    def update_rect(x, stack, one, rows, cols, skip=()):
        base = near_at(one)

        def body(i, carry):
            a = rows[0] + i
            for e in cols:
                two = (a + 1) * 3 + e + 1
                at = (a - one[0] + 1) * 3 + e - one[1] + 1
                store[x, at] = store[x, at] - lax.dot_general(
                    stack[base, 0 : 3 * slots], stack[two, slots : 4 * slots],
                    (((0,), (0,)), ((), ())), preferred_element_type=jnp.float32,
                )
            return carry

        lax.fori_loop(0, len(rows), body, 0)

    def update_parent(x, stack, one, two):
        at = near_at((two[0] - one[0], two[1] - one[1]))
        change = lax.dot_general(
            stack[near_at(one), 0 : 3 * slots], stack[near_at(two), slots : 4 * slots],
            (((0,), (0,)), ((), ())), preferred_element_type=jnp.float32,
        )
        store[x, at, low:] = store[x, at, low:] - change[low:]

    def panel_maker(x, hooks=()):
        red = counts[x // 2, x % 2]
        row_ids = lax.broadcasted_iota(jnp.int32, (slots, slots), 0)
        col_ids = lax.broadcasted_iota(jnp.int32, (slots, slots), 1)
        masked = jnp.where((row_ids < red) & (col_ids + low >= red), interp[x], 0.0)
        wide_rows = lax.broadcasted_iota(jnp.int32, (slots, points), 0)
        wide_cols = lax.broadcasted_iota(jnp.int32, (slots, points), 1)
        reduce = (wide_rows == wide_cols).astype(jnp.float32) - jnp.concatenate(
            [jnp.zeros((slots, low), jnp.float32), masked], axis=1
        )
        reduced = jnp.dot(reduce, store[x, 4], precision=EXACT)
        block = lax.dot_general(reduced, reduce, (((1,), (1,)), ((), ())), precision=EXACT)
        block = jnp.where(
            (row_ids < red) & (col_ids < red), block, (row_ids == col_ids).astype(jnp.float32)
        )
        block = 0.5 * (block + block.T)
        inverse = factor_inverse(block, hooks)
        inverse = jnp.where(col_ids < red, inverse, 0.0)
        whole_high, whole_low = split(jnp.dot(inverse, reduce, precision=EXACT))
        left = jnp.concatenate([whole_high, whole_high, whole_low], axis=1)

        def make(k):
            at = near_at(k)
            high, less = split(store[x, at])
            value = dot(left, jnp.concatenate([high, less, high], axis=0))
            if k == (0, 0):
                value = jnp.where(wide_cols >= red, value, 0.0)
            panels[x, at] = value
            make_stack(value, stacks.at[x % 2, at])

        return make

    def wait_load(i):
        loads[i].wait()
        loads[4 + i].wait()

    mine = [stacks.at[0], stacks.at[1], stacks.at[0], stacks.at[1]]
    from_right, from_down, from_left, other = (shared.at[i] for i in range(4))

    wait_load(0)
    make = panel_maker(0)
    pl.semaphore_wait(barrier, sum(has[way].astype(jnp.int32) for way in has))
    order = TRAVEL["l0"] + [(-1, 1), (0, 1), (1, 1)]
    for k in order:
        make(k)
        if k in TRAVEL["l0"]:
            send("l0", k, panels.at[0, near_at(k)], "left")
        if k in TRAVEL["u0"]:
            send("u0", k, panels.at[0, near_at(k)], "up")
    wait_load(1)
    wait_load(2)
    wait_load(3)
    update_rect(1, mine[0], (0, 1), (-1, 0, 1), (0, 1))
    update_rect(2, mine[0], (1, 0), (0, 1), (-1, 0, 1))
    update_rect(3, mine[0], (1, 1), (0, 1), (0, 1))
    update_parent(0, mine[0], (0, 0), (0, 0))

    @pl.when(has["right"])
    def _():
        receive("l0", (0, -1), from_right)
        update(1, from_right, (0, -1), [(0, -1)])

    send("d0", (0, -1), arrived.at[slot("l0", (0, -1))], "up", "right")
    make = panel_maker(1)
    for k in TRAVEL["l0"][1:]:
        @pl.when(has["right"])
        def _(k=k):
            receive("l0", k, from_right)
            update(1, from_right, (0, -1), [k])

        if k in TRAVEL["d0"]:
            send("d0", k, arrived.at[slot("l0", k)], "up", "right")
        k = (k[0], k[1] + 1)
        make(k)
        send("r1", k, panels.at[1, near_at(k)], "right")
        if k in TRAVEL["u1"]:
            send("u1", k, panels.at[1, near_at(k)], "up")
    for k in ((0, 0), (-1, -1), (0, -1), (1, -1)):
        make(k)
        if k in TRAVEL["r1"]:
            send("r1", k, panels.at[1, near_at(k)], "right")
        if k in TRAVEL["u1"]:
            send("u1", k, panels.at[1, near_at(k)], "up")
    update_rect(2, mine[1], (1, -1), (0, 1), (-1, 0))
    update_rect(3, mine[1], (1, 0), (0, 1), (-1, 0, 1))
    update_parent(0, mine[1], (0, -1), (0, -1))
    update_parent(1, mine[1], (0, 0), (0, -1))
    update_parent(1, mine[1], (0, 0), (0, 0))

    @pl.when(has["down"])
    def _():
        for k in TRAVEL["u0"]:
            receive("u0", k, from_down)
        update_rect(2, from_down, (-1, 0), (-1, 0), (-1, 0, 1))
        update_rect(3, from_down, (-1, 1), (-1, 0), (0, 1))
        receive("u1", (-1, -1), from_down)
        update(2, from_down, (-1, -1), [(-1, -1)])

    @pl.when(has["left"])
    def _():
        receive("r1", (1, 1), from_left)
        update(2, from_left, (1, 1), [(1, 1)])
        receive("r1", (-1, 1), from_left)

    send("d1", (-1, 1), arrived.at[slot("r1", (-1, 1))], "up", "left")

    @pl.when(has["right"])
    def _():
        update_rect(3, from_right, (1, -1), (0, 1), (-1, 0))

    @pl.when(has["down"] & has["left"])
    def _():
        receive("d1", (-1, 1), other)
        update(2, other, (-1, 1), [(-1, 1)])

    def forward():
        k = (-1, 0)
        pl.when(has["left"])(lambda: receive("r1", k, from_left))
        send("d1", k, arrived.at[slot("r1", k)], "up", "left")

    make = panel_maker(2, [(3, forward)])

    @pl.when(has["down"])
    def _():
        for k in TRAVEL["u1"][1:]:
            receive("u1", k, from_down)
        update(2, from_down, (-1, -1), [(-1, 0), (0, -1), (0, 0)])
        update_rect(3, from_down, (-1, 0), (-1, 0), (-1, 0, 1))

    @pl.when(has["left"])
    def _():
        receive("r1", (1, 0), from_left)
        update(2, from_left, (1, 1), [(1, 0)])

    @pl.when(has["down"] & has["left"])
    def _():
        receive("d1", (-1, 0), other)
        update(2, other, (-1, 1), [(-1, 0)])

    def finish(k):
        make(k)
        if k in TRAVEL["l2"]:
            send("l2", k, panels.at[2, near_at(k)], "left")
        if k in TRAVEL["v2"]:
            send("v2", k, panels.at[2, near_at(k)], "down")

    finish((0, -1))
    finish((0, 0))
    finish((0, 1))
    for k, one, two in (((0, 1), (-1, 0), (1, 0)), ((0, 0), (-1, -1), (1, -1))):
        @pl.when(has["left"])
        def _(k=k):
            receive("r1", k, from_left)
            update(2, from_left, (1, 1), [k])

        send("d1", k, arrived.at[slot("r1", k)], "up", "left")
        finish(one)

        @pl.when(has["down"] & has["left"])
        def _(k=k):
            receive("d1", k, other)
            update(2, other, (-1, 1), [k])

        finish(two)
    finish((1, 1))
    finish((-1, 1))
    update_rect(3, mine[2], (0, 1), (-1, 0, 1), (0, 1))

    @pl.when(has["left"])
    def _():
        update_parent(0, from_left, (0, 1), (0, 1))

    @pl.when(has["down"] & has["right"])
    def _():
        for k in TRAVEL["d0"]:
            receive("d0", k, other)
        update_rect(3, other, (-1, -1), (-1, 0), (-1, 0))

    @pl.when(has["right"])
    def _():
        receive("l2", (0, -1), from_right)
        update(3, from_right, (0, -1), [(0, -1)])

    make = panel_maker(3)
    update_parent(0, mine[2], (-1, 0), (-1, 0))
    update_parent(1, mine[2], (-1, 1), (-1, 0))
    update_parent(1, mine[2], (-1, 1), (-1, 1))
    update_parent(2, mine[2], (0, 0), (-1, 0))
    update_parent(2, mine[2], (0, 0), (-1, 1))
    update_parent(2, mine[2], (0, 0), (0, 0))
    for k in TRAVEL["l2"][1:]:
        @pl.when(has["right"])
        def _(k=k):
            receive("l2", k, from_right)
            update(3, from_right, (0, -1), [k])

        if k in TRAVEL["d2"]:
            send("d2", k, arrived.at[slot("l2", k)], "down", "right")
        k = (k[0], k[1] + 1)
        make(k)
        if k in TRAVEL["r3"]:
            send("r3", k, panels.at[3, near_at(k)], "right")
        if k in TRAVEL["v3"]:
            send("v3", k, panels.at[3, near_at(k)], "down")
    for k in ((1, -1), (0, 0), (-1, -1), (0, -1)):
        make(k)
        if k in TRAVEL["v3"]:
            send("v3", k, panels.at[3, near_at(k)], "down")

    places = [(-1, -1), (-1, 0), (0, -1), (0, 0)]
    for x in range(4):
        for y in range(x + 1):
            update_parent(x, mine[3], places[x], places[y])

    @pl.when(has["right"])
    def _():
        update_parent(1, from_right, (-1, -1), (-1, -1))

    @pl.when(has["up"])
    def _():
        receive("v2", (1, 0), from_down)
        receive("v2", (1, 1), from_down)
        update_parent(0, from_down, (1, 0), (1, 0))
        update_parent(1, from_down, (1, 1), (1, 0))
        update_parent(1, from_down, (1, 1), (1, 1))

    @pl.when(has["up"] & has["right"])
    def _():
        receive("d2", (1, -1), other)
        update_parent(1, other, (1, -1), (1, -1))

    def keep(x, y):
        row_ids = lax.broadcasted_iota(jnp.int32, (slots, slots), 0) + low
        col_ids = lax.broadcasted_iota(jnp.int32, (slots, slots), 1) + low
        return (row_ids >= counts[x // 2, x % 2]) & (col_ids >= counts[y // 2, y % 2])

    for _, copy in pulls.values():
        copy.wait()

    @pl.when(has["left"])
    def _():
        for k in TRAVEL["r3"]:
            receive("r3", k, from_left)

    send("d3", (1, 1), arrived.at[slot("r3", (1, 1))], "down", "left")

    @pl.when(has["left"])
    def _():
        update_parent(0, from_left, (-1, 1), (-1, 1))
        update_parent(2, from_left, (0, 1), (-1, 1))
        update_parent(2, from_left, (0, 1), (0, 1))

    @pl.when(has["up"])
    def _():
        receive("v3", (1, -1), from_down)
        receive("v3", (1, 0), from_down)
        update_parent(0, from_down, (1, -1), (1, -1))
        update_parent(1, from_down, (1, 0), (1, -1))
        update_parent(1, from_down, (1, 0), (1, 0))

    @pl.when(has["up"] & has["left"])
    def _():
        receive("d3", (1, 1), other)
        update_parent(0, other, (1, 1), (1, 1))

    for x in range(4):
        for y in range(x + 1):
            at = near_at((y // 2 - x // 2, y % 2 - x % 2))
            block = jnp.where(keep(x, y), store[x, at, low:][:, low:], 0.0)
            out[x * slots : (x + 1) * slots, y * slots : (y + 1) * slots] = block
            if y < x:
                skew = pulled[pulls[y, x][0]][:, low:] - pulled[pulls[x, y][0]][:, low:].T
                out[y * slots : (y + 1) * slots, x * slots : (x + 1) * slots] = (
                    jnp.where(keep(y, x), skew, 0.0) + block.T
                )
    for copy, way, and_also in sent:
        if and_also is None:
            pl.when(has[way])(copy.wait_send)
        else:
            pl.when(has[way] & has[and_also])(copy.wait_send)


def from_partner(value, axis):
    pairs = [(source, source ^ 1) for source in range(lax.axis_size(axis))]
    return lax.ppermute(value, axis, pairs)


def local(near, interp, red_count, owner_flip):
    points, slots = near.shape[-1], interp.shape[-1]
    boxes = near.reshape(4, 9, points, points)
    any_space = pl.BlockSpec(memory_space=pl.ANY)
    parent = pl.pallas_call(
        functools.partial(kernel, (lax.axis_size("row"), lax.axis_size("col"))),
        out_shape=jax.ShapeDtypeStruct((4 * slots, 4 * slots), jnp.float32),
        in_specs=[any_space, any_space, pl.BlockSpec(memory_space=pltpu.SMEM)],
        out_specs=pl.BlockSpec(memory_space=pltpu.VMEM),
        scratch_shapes=[
            pltpu.VMEM((4, 9, points, points), jnp.float32),
            pltpu.VMEM((4, slots, slots), jnp.float32),
            pltpu.VMEM((4, 9, slots, points), jnp.float32),
            pltpu.VMEM((2, 9, 4 * slots, points), jnp.bfloat16),
            pltpu.VMEM((COUNT, slots, points), jnp.float32),
            pltpu.VMEM((4, 9, 4 * slots, points), jnp.bfloat16),
            pltpu.VMEM((12, slots, points), jnp.float32),
            pltpu.SemaphoreType.DMA((COUNT,)),
            pltpu.SemaphoreType.DMA((COUNT,)),
            pltpu.SemaphoreType.DMA((20,)),
        ],
        compiler_params=pltpu.CompilerParams(
            vmem_limit_bytes=60 * 2**20, collective_id=0, has_side_effects=True
        ),
        name="skeletonize",
    )(boxes, interp, red_count)
    flip = owner_flip[0, 0]
    parent = jnp.where(flip[0] == 1, from_partner(parent, "row"), parent)
    parent = jnp.where(flip[1] == 1, from_partner(parent, "col"), parent)
    return parent[None, None]


def solution(mesh):
    in_specs = (
        P("row", "col", None, None, None, None),
        P("row", "col", None, None),
        P("row", "col"),
        P("row", "col", None),
    )
    out_specs = P("row", "col", None, None)
    return jax.shard_map(local, mesh=mesh, in_specs=in_specs, out_specs=out_specs, check_vma=False)
```

```python
import functools

import jax
import jax.numpy as jnp
from jax import lax
from jax.experimental import pallas as pl
from jax.experimental.pallas import tpu as pltpu
from jax.sharding import PartitionSpec as P

EXACT = lax.Precision.HIGHEST
GROUP = 8
BLOCK = 32
MESH = pl.DeviceIdType.MESH

FULL = [(a, e) for a in (-1, 0, 1) for e in (-1, 0, 1)]
TRAVEL = {
    "l0": [(0, -1), (1, 0), (-1, 0), (-1, -1), (1, -1), (0, 0)],
    "u0": [(-1, 0), (-1, -1), (0, -1), (0, 0), (-1, 1), (0, 1)],
    "d0": [(0, -1), (-1, 0), (-1, -1), (0, 0)],
    "r1": [(1, 1), (-1, 1), (-1, 0), (1, 0), (0, 1), (0, 0)],
    "u1": [(-1, -1), (-1, 0), (-1, 1), (0, -1), (0, 0), (0, 1)],
    "d1": [(-1, 1), (-1, 0), (0, 1), (0, 0)],
    "l2": [(0, -1), (0, 0), (-1, 0), (1, 0), (-1, -1), (1, -1)],
    "v2": [(1, 0), (1, 1)],
    "d2": [(1, -1)],
    "r3": [(-1, 1), (0, 1), (1, 1)],
    "v3": [(1, -1), (1, 0)],
    "d3": [(1, 1)],
}
FIRST = {}
COUNT = 0
for _name, _panels in TRAVEL.items():
    FIRST[_name] = COUNT
    COUNT += len(_panels)


STRIPS = {
    "A3": [(3, 0), (3, 1), (3, 2), (3, 3)],
    "A2": [(2, 0), (2, 1), (2, 2), (0, 0)],
    "A1": [(1, 0), (1, 1)],
    "E3": [(0, 3), (1, 3), (2, 3), (0, 1)],
    "E2": [(0, 2), (1, 2)],
}


def strip_places(slots):
    places, total = {}, 0
    for name, blocks in STRIPS.items():
        width = -(-len(blocks) * slots // 128) * 128
        places[name] = (total, width)
        total += width
    return places, total


PACKED = {("l0", (0, 0)), ("r1", (0, 1)), ("r1", (0, 0)), ("d0", (0, 0)), ("d1", (0, 1)), ("d1", (0, 0))}
PACKED |= {(name, k) for name in ("l2", "r3", "d2", "d3") for k in TRAVEL[name]} - {("l2", (0, -1))}
PACKED = sorted(PACKED)


def slot(name, k):
    return FIRST[name] + TRAVEL[name].index(k)


def near_at(k):
    return (k[0] + 1) * 3 + k[1] + 1


def split(value):
    high = value.astype(jnp.bfloat16)
    low = (value - high.astype(jnp.float32)).astype(jnp.bfloat16)
    return high, low


def dot(left, right):
    return jnp.dot(left, right, preferred_element_type=jnp.float32)


def diagonal_inverse(block):
    size = block.shape[0]
    rows = lax.broadcasted_iota(jnp.int32, (size, size), 0)
    cols = lax.broadcasted_iota(jnp.int32, (size, size), 1)
    eye = (rows == cols).astype(jnp.float32)
    wide = jnp.concatenate([block, eye, jnp.zeros((size, 128 - 2 * size), jnp.float32)], axis=1)
    row_ids = lax.broadcasted_iota(jnp.int32, (size, 128), 0)
    scale = jnp.ones((size, 128), jnp.float32)
    for start in range(0, size, GROUP):
        columns = [
            jnp.broadcast_to(wide[:, start + q : start + q + 1], (size, 128)) for q in range(GROUP)
        ]
        for q in range(GROUP):
            at = start + q
            pivot = columns[q][at : at + 1, :]
            inverse = 1.0 / pivot
            below = jnp.where(row_ids > at, columns[q], 0.0)
            scale = jnp.where(row_ids == at, lax.rsqrt(pivot), scale)
            wide = wide - below * (wide[at : at + 1, :] * inverse)
            for p in range(q + 1, GROUP):
                columns[p] = columns[p] - below * (columns[p][at : at + 1, :] * inverse)
    return (wide * scale)[:, size : 2 * size]


def factor_inverse(matrix, hooks=()):
    size = matrix.shape[0]
    rows = lax.broadcasted_iota(jnp.int32, (size, size), 0)
    cols = lax.broadcasted_iota(jnp.int32, (size, size), 1)
    rest = matrix
    right = (rows == cols).astype(jnp.float32)
    done = []
    for start in range(0, size, BLOCK):
        inverse = diagonal_inverse(rest[:BLOCK, :BLOCK])
        top_right = jnp.dot(inverse, right[:BLOCK], precision=EXACT)
        done.append(top_right)
        if start + BLOCK < size:
            top = jnp.dot(inverse, rest[:BLOCK, BLOCK:], precision=EXACT)
            top_t = top.T
            rest = rest[BLOCK:, BLOCK:] - jnp.dot(top_t, top, precision=EXACT)
            right = right[BLOCK:] - jnp.dot(top_t, top_right, precision=EXACT)
        for at, hook in hooks:
            if at == start // BLOCK:
                hook()
    return jnp.concatenate(done, axis=0)


def kernel(sizes, near, interp_all, counts, flip, out, store, interp, panels, tops, stacks, arrived,
           packed, small, shared, pulled, own, first_got, chosen, last_got, send_sem, recv_sem, load_sem, strip_send,
           strip_recv):
    n_row, n_col = sizes
    points, slots = store.shape[-1], interp.shape[-1]
    low = points - slots
    row, col = lax.axis_index("row"), lax.axis_index("col")
    has = {
        "up": row > 0, "down": row < n_row - 1, "left": col > 0, "right": col < n_col - 1,
    }
    where_to = {
        "up": {"row": row - 1, "col": col}, "down": {"row": row + 1, "col": col},
        "left": {"row": row, "col": col - 1}, "right": {"row": row, "col": col + 1},
    }
    row_partner = {"row": row + 1 - 2 * lax.rem(row, 2), "col": col}
    col_partner = {"row": row, "col": col + 1 - 2 * lax.rem(col, 2)}

    loads = [pltpu.make_async_copy(near.at[i], store.at[i], load_sem.at[i]) for i in range(4)]
    loads += [
        pltpu.make_async_copy(interp_all.at[i // 2, i % 2], interp.at[i], load_sem.at[4 + i])
        for i in range(4)
    ]
    pulls = {}
    for y in range(4):
        for x in range(y):
            for one, two in ((x, y), (y, x)):
                k = near_at((two // 2 - one // 2, two % 2 - one % 2))
                n = len(pulls)
                pulls[one, two] = n, pltpu.make_async_copy(
                    near.at[one, k, pl.ds(low, slots), :], pulled.at[n], load_sem.at[8 + n]
                )
    for _, copy in pulls.values():
        copy.start()
    for i in (0, 4, 1, 5, 2, 6, 3, 7):
        loads[i].start()

    barrier = pltpu.get_barrier_semaphore()
    for way in has:
        @pl.when(has[way])
        def _(way=way):
            pl.semaphore_signal(barrier, inc=1, device_id=where_to[way], device_id_type=MESH)

    sent = []

    lanes = points // 2
    tail = points - low - lanes
    piece = slots * tail // lanes

    def pack(value, ref):
        ref[0:slots] = value[:, lanes:]
        lane_ids = lax.broadcasted_iota(jnp.int32, (piece, lanes), 1)
        folded = jnp.zeros((piece, lanes), jnp.float32)
        for i in range(slots // piece):
            part = pltpu.roll(value[i * piece : (i + 1) * piece, :lanes], (i * tail - low) % lanes, 1)
            inside = (lane_ids >= i * tail) & (lane_ids < (i + 1) * tail)
            folded = jnp.where(inside, part, folded)
        ref[slots:] = folded

    def unpack(ref):
        parts = [pltpu.roll(ref[slots:], (low - i * tail) % lanes, 1) for i in range(slots // piece)]
        front = jnp.concatenate(parts, axis=0)
        lane_ids = lax.broadcasted_iota(jnp.int32, (slots, lanes), 1)
        return jnp.concatenate([jnp.where(lane_ids >= low, front, 0.0), ref[0:slots]], axis=1)

    def landing(name, k):
        if (name, k) in PACKED:
            return small.at[PACKED.index((name, k))]
        return arrived.at[slot(name, k)]

    def copy_of(name, k, source, way):
        i = slot(name, k)
        return pltpu.make_async_remote_copy(
            src_ref=source, dst_ref=landing(name, k), send_sem=send_sem.at[i],
            recv_sem=recv_sem.at[i], device_id=where_to[way], device_id_type=MESH,
        )

    def send(name, k, source, way, and_also=None):
        if source is None:
            source = panels.at[int(name[1]), near_at(k)]
            if (name, k) in PACKED:
                staged = packed.at[PACKED.index((name, k))]
                pl.when(has[way])(lambda: pack(source[...], staged))
                source = staged
        copy = copy_of(name, k, source, way)
        sent.append((copy, way, and_also))
        if and_also is None:
            pl.when(has[way])(copy.start)
        else:
            pl.when(has[way] & has[and_also])(copy.start)

    def make_stack(value, ref):
        high, less = split(value)
        ref[0:slots] = high
        ref[slots : 2 * slots] = high
        ref[2 * slots : 3 * slots] = less
        ref[3 * slots : 4 * slots] = high

    def arrive(name, k):
        i = slot(name, k)
        pltpu.make_async_remote_copy(
            src_ref=landing(name, k), dst_ref=landing(name, k), send_sem=send_sem.at[i],
            recv_sem=recv_sem.at[i], device_id=where_to["up"], device_id_type=MESH,
        ).wait_recv()
        return unpack(landing(name, k)) if (name, k) in PACKED else arrived[i]

    def receive(name, k, stack):
        make_stack(arrive(name, k), stack.at[near_at(k)])

    def product(stack, one, two):
        return lax.dot_general(
            stack[near_at(one), 0 : 3 * slots], stack[near_at(two), slots : 4 * slots],
            (((0,), (0,)), ((), ())), preferred_element_type=jnp.float32,
        )

    def update(x, stack, one, twos):
        for two in twos:
            at = near_at((two[0] - one[0], two[1] - one[1]))
            store[x, at] = store[x, at] - product(stack, one, two)

    def update_rect(x, stack, one, rows, cols):
        base = near_at(one)

        def body(i, carry):
            a = rows[0] + i
            for e in cols:
                two = (a + 1) * 3 + e + 1
                at = (a - one[0] + 1) * 3 + e - one[1] + 1
                store[x, at] = store[x, at] - lax.dot_general(
                    stack[base, 0 : 3 * slots], stack[two, slots : 4 * slots],
                    (((0,), (0,)), ((), ())), preferred_element_type=jnp.float32,
                )
            return carry

        lax.fori_loop(0, len(rows), body, 0)

    def update_parent(x, stack, one, two):
        at = near_at((two[0] - one[0], two[1] - one[1]))
        store[x, at, low:] = store[x, at, low:] - product(stack, one, two)[low:]

    def panel_maker(x, hooks=()):
        red = counts[x // 2, x % 2]
        row_ids = lax.broadcasted_iota(jnp.int32, (slots, slots), 0)
        col_ids = lax.broadcasted_iota(jnp.int32, (slots, slots), 1)
        masked = jnp.where((row_ids < red) & (col_ids + low >= red), interp[x], 0.0)
        wide_rows = lax.broadcasted_iota(jnp.int32, (slots, points), 0)
        wide_cols = lax.broadcasted_iota(jnp.int32, (slots, points), 1)
        reduce = (wide_rows == wide_cols).astype(jnp.float32) - jnp.concatenate(
            [jnp.zeros((slots, low), jnp.float32), masked], axis=1
        )
        reduced = jnp.dot(reduce, store[x, 4], precision=EXACT)
        block = lax.dot_general(reduced, reduce, (((1,), (1,)), ((), ())), precision=EXACT)
        block = jnp.where(
            (row_ids < red) & (col_ids < red), block, (row_ids == col_ids).astype(jnp.float32)
        )
        block = 0.5 * (block + block.T)
        inverse = factor_inverse(block, hooks)
        inverse = jnp.where(col_ids < red, inverse, 0.0)
        whole_high, whole_low = split(jnp.dot(inverse, reduce, precision=EXACT))
        tops[x] = jnp.concatenate([whole_high, whole_high, whole_low], axis=1)

        def make(k):
            at = near_at(k)
            high, less = split(store[x, at])
            value = dot(tops[x], jnp.concatenate([high, less, high], axis=0))
            if k == (0, 0):
                value = jnp.where(wide_cols >= red, value, 0.0)
            panels[x, at] = value
            make_stack(value, stacks.at[x % 2, at])

        return make

    def keep(x, y):
        row_ids = lax.broadcasted_iota(jnp.int32, (slots, slots), 0) + low
        col_ids = lax.broadcasted_iota(jnp.int32, (slots, slots), 1) + low
        return (row_ids >= counts[x // 2, x % 2]) & (col_ids >= counts[y // 2, y % 2])

    places, _ = strip_places(slots)
    strip_at = list(STRIPS)

    def strip_copy(name, first_hop):
        along_row = first_hop == (name[0] == "A")
        i = strip_at.index(name) + (0 if first_hop else len(strip_at))
        first, width = places[name]
        source, target = (own, first_got) if first_hop else (chosen, last_got)
        return pltpu.make_async_remote_copy(
            src_ref=source.at[:, pl.ds(first, width)], dst_ref=target.at[:, pl.ds(first, width)],
            send_sem=strip_send.at[i], recv_sem=strip_recv.at[i],
            device_id=row_partner if along_row else col_partner, device_id_type=MESH,
        )

    def pick(name, first_hop):
        first, width = places[name]
        view = (slice(None), slice(first, first + width))
        axis = 0 if first_hop == (name[0] == "A") else 1
        flipped = jnp.full((slots, width), flip[0, 0, axis], jnp.int32) == 1
        if first_hop:
            return jnp.where(flipped, first_got[view], own[view])
        return jnp.where(flipped, last_got[view], chosen[view])

    def start_strip(name):
        for at, (x, y) in enumerate(STRIPS[name]):
            first = places[name][0] + at * slots
            at = near_at((y // 2 - x // 2, y % 2 - x % 2))
            if name[0] == "A":
                block = store[x, at, low:][:, low:]
            else:
                block = pulled[pulls[x, y][0]][:, low:] - pulled[pulls[y, x][0]][:, low:].T
            own[:, first : first + slots] = jnp.where(keep(x, y), block, 0.0)
        end = places[name][0] + len(STRIPS[name]) * slots
        if end < sum(places[name]):
            own[:, end : sum(places[name])] = jnp.zeros((slots, sum(places[name]) - end), jnp.float32)
        strip_copy(name, True).start()

    def pass_strip(name):
        strip_copy(name, True).wait_recv()
        first, width = places[name]
        chosen[:, first : first + width] = pick(name, True)
        strip_copy(name, False).start()

    def end_strip(name):
        strip_copy(name, False).wait_recv()
        value = pick(name, False)
        for at, (x, y) in enumerate(STRIPS[name]):
            block = value[:, at * slots : (at + 1) * slots]
            rows, cols = slice(x * slots, (x + 1) * slots), slice(y * slots, (y + 1) * slots)
            out[rows, cols] = block
            if name[0] == "A" and y < x:
                out[cols, rows] = out[cols, rows] + block.T

    def wait_load(i):
        loads[i].wait()
        loads[4 + i].wait()

    mine = [stacks.at[0], stacks.at[1], stacks.at[0], stacks.at[1]]
    from_right, from_down, from_left, other = (shared.at[i] for i in range(4))

    for _, copy in pulls.values():
        copy.wait()
    pl.semaphore_wait(barrier, sum(has[way].astype(jnp.int32) for way in has))
    start_strip("E3")
    wait_load(0)
    make = panel_maker(0)
    for k in TRAVEL["l0"] + [(-1, 1), (0, 1), (1, 1)]:
        make(k)
        if k in TRAVEL["l0"]:
            send("l0", k, None, "left")
        if k in TRAVEL["u0"]:
            send("u0", k, None, "up")
    wait_load(1)
    wait_load(2)
    wait_load(3)
    update_rect(1, mine[0], (0, 1), (-1, 0, 1), (0, 1))
    update_rect(2, mine[0], (1, 0), (0, 1), (-1, 0, 1))
    update_rect(3, mine[0], (1, 1), (0, 1), (0, 1))
    update_parent(0, mine[0], (0, 0), (0, 0))

    @pl.when(has["right"])
    def _():
        receive("l0", (0, -1), from_right)
        update(1, from_right, (0, -1), [(0, -1)])

    send("d0", (0, -1), landing("l0", (0, -1)), "up", "right")
    make_one = panel_maker(1)

    def finish_one(k):
        make_one(k)
        if k in TRAVEL["r1"]:
            send("r1", k, None, "right")
        if k in TRAVEL["u1"]:
            send("u1", k, None, "up")

    def step_one(k):
        @pl.when(has["right"])
        def _():
            receive("l0", k, from_right)
            update(1, from_right, (0, -1), [k])

        if k in TRAVEL["d0"]:
            send("d0", k, landing("l0", k), "up", "right")
        finish_one((k[0], k[1] + 1))

    step_one((1, 0))
    step_one((-1, 0))
    finish_one((-1, -1))
    finish_one((1, -1))
    finish_one((0, -1))
    update(2, mine[1], (1, -1), [(1, -1), (0, -1)])
    update_parent(0, mine[1], (0, -1), (0, -1))

    @pl.when(has["down"])
    def _():
        for k in TRAVEL["u0"]:
            receive("u0", k, from_down)
        update_rect(2, from_down, (-1, 0), (-1, 0), (-1, 0, 1))
        update_rect(3, from_down, (-1, 1), (-1, 0), (0, 1))
        receive("u1", (-1, -1), from_down)
        update(2, from_down, (-1, -1), [(-1, -1)])

    @pl.when(has["left"])
    def _():
        receive("r1", (1, 1), from_left)
        update(2, from_left, (1, 1), [(1, 1)])
        arrive("r1", (-1, 1))

    send("d1", (-1, 1), landing("r1", (-1, 1)), "up", "left")

    @pl.when(has["down"] & has["left"])
    def _():
        receive("d1", (-1, 1), other)
        update(2, other, (-1, 1), [(-1, 1)])

    def pass_on(k):
        pl.when(has["left"])(lambda: receive("r1", k, from_left))
        send("d1", k, landing("r1", k), "up", "left")

    def last_one():
        step_one((0, 0))
        finish_one((0, 0))

    make_two = panel_maker(2, [
        (0, lambda: step_one((-1, -1))), (1, lambda: step_one((1, -1))), (2, last_one),
        (3, lambda: pass_on((-1, 0))),
    ])

    @pl.when(has["left"])
    def _():
        receive("r1", (1, 0), from_left)
        update(2, from_left, (1, 1), [(1, 0)])

    @pl.when(has["down"] & has["left"])
    def _():
        receive("d1", (-1, 0), other)
        update(2, other, (-1, 1), [(-1, 0)])

    def finish_two(k):
        make_two(k)
        if k in TRAVEL["l2"]:
            send("l2", k, None, "left")
        if k in TRAVEL["v2"]:
            send("v2", k, None, "down")

    finish_two((0, -1))
    finish_two((0, 0))
    pass_on((0, 1))

    @pl.when(has["left"])
    def _():
        update(2, from_left, (1, 1), [(0, 1)])

    finish_two((-1, 0))

    @pl.when(has["down"])
    def _():
        for k in TRAVEL["u1"][1:]:
            receive("u1", k, from_down)
        update(2, from_down, (-1, -1), [(-1, 0), (0, -1), (0, 0)])

    update(2, mine[1], (1, -1), [(1, 0), (0, 0)])
    pass_on((0, 0))

    @pl.when(has["down"] & has["left"])
    def _():
        receive("d1", (0, 1), other)
        update(2, other, (-1, 1), [(0, 1)])

    finish_two((1, 0))

    @pl.when(has["left"])
    def _():
        update(2, from_left, (1, 1), [(0, 0)])
        update_parent(0, from_left, (0, 1), (0, 1))

    finish_two((-1, -1))

    @pl.when(has["down"] & has["left"])
    def _():
        receive("d1", (0, 0), other)
        update(2, other, (-1, 1), [(0, 0)])

    finish_two((1, -1))
    finish_two((1, 1))
    finish_two((0, 1))
    finish_two((-1, 1))
    update_rect(3, mine[2], (0, 1), (-1, 0, 1), (0, 1))
    update_rect(3, mine[1], (1, 0), (0, 1), (-1, 0, 1))
    update_parent(1, mine[1], (0, 0), (0, -1))
    update_parent(1, mine[1], (0, 0), (0, 0))

    @pl.when(has["right"])
    def _():
        update_rect(3, from_right, (1, -1), (0, 1), (-1, 0))

    @pl.when(has["down"])
    def _():
        update_rect(3, from_down, (-1, 0), (-1, 0), (-1, 0, 1))

    @pl.when(has["down"] & has["right"])
    def _():
        for k in TRAVEL["d0"]:
            receive("d0", k, other)
        update_rect(3, other, (-1, -1), (-1, 0), (-1, 0))

    @pl.when(has["right"])
    def _():
        receive("l2", (0, -1), from_right)
        update(3, from_right, (0, -1), [(0, -1)])

    start_strip("E2")
    make_three = panel_maker(3)
    pass_strip("E3")
    update_parent(0, mine[2], (-1, 0), (-1, 0))
    update_parent(1, mine[2], (-1, 1), (-1, 0))
    update_parent(1, mine[2], (-1, 1), (-1, 1))
    update_parent(2, mine[2], (0, 0), (-1, 0))
    update_parent(2, mine[2], (0, 0), (-1, 1))
    update_parent(2, mine[2], (0, 0), (0, 0))
    end_strip("E3")

    def finish_three(k):
        make_three(k)
        if k in TRAVEL["r3"]:
            send("r3", k, None, "right")
        if k in TRAVEL["v3"]:
            send("v3", k, None, "down")

    for k in TRAVEL["l2"][1:]:
        @pl.when(has["right"])
        def _(k=k):
            receive("l2", k, from_right)
            update(3, from_right, (0, -1), [k])

        if k in TRAVEL["d2"]:
            send("d2", k, landing("l2", k), "down", "right")
        finish_three((k[0], k[1] + 1))
    for k in ((1, -1), (0, 0), (-1, -1), (0, -1)):
        finish_three(k)

    corners = [(-1, -1), (-1, 0), (0, -1), (0, 0)]
    for y in range(4):
        update_parent(3, mine[3], corners[3], corners[y])
    start_strip("A3")
    pass_strip("E2")
    for x in range(3):
        for y in range(x + 1):
            update_parent(x, mine[3], corners[x], corners[y])
    pass_strip("A3")

    @pl.when(has["right"])
    def _():
        update_parent(1, from_right, (-1, -1), (-1, -1))

    @pl.when(has["up"])
    def _():
        receive("v2", (1, 0), from_down)
        receive("v2", (1, 1), from_down)
        update_parent(0, from_down, (1, 0), (1, 0))
        update_parent(1, from_down, (1, 1), (1, 0))
        update_parent(1, from_down, (1, 1), (1, 1))
        receive("v3", (1, -1), from_down)
        receive("v3", (1, 0), from_down)
        update_parent(0, from_down, (1, -1), (1, -1))
        update_parent(1, from_down, (1, 0), (1, -1))
        update_parent(1, from_down, (1, 0), (1, 0))

    @pl.when(has["up"] & has["right"])
    def _():
        receive("d2", (1, -1), other)
        update_parent(1, other, (1, -1), (1, -1))

    start_strip("A1")

    @pl.when(has["left"])
    def _():
        for k in TRAVEL["r3"]:
            receive("r3", k, from_left)

    send("d3", (1, 1), landing("r3", (1, 1)), "down", "left")

    @pl.when(has["left"])
    def _():
        update_parent(0, from_left, (-1, 1), (-1, 1))
        update_parent(2, from_left, (0, 1), (-1, 1))
        update_parent(2, from_left, (0, 1), (0, 1))

    pass_strip("A1")

    @pl.when(has["up"] & has["left"])
    def _():
        receive("d3", (1, 1), other)
        update_parent(0, other, (1, 1), (1, 1))

    start_strip("A2")
    pass_strip("A2")
    for name in ("E2", "A3", "A1", "A2"):
        end_strip(name)
    for copy, way, and_also in sent:
        if and_also is None:
            pl.when(has[way])(copy.wait_send)
        else:
            pl.when(has[way] & has[and_also])(copy.wait_send)
    for name in STRIPS:
        strip_copy(name, True).wait_send()
        strip_copy(name, False).wait_send()


def local(near, interp, red_count, owner_flip):
    points, slots = near.shape[-1], interp.shape[-1]
    boxes = near.reshape(4, 9, points, points)
    strip_width = strip_places(slots)[1]
    small_rows = 2 * slots * slots // points
    any_space = pl.BlockSpec(memory_space=pl.ANY)
    parent = pl.pallas_call(
        functools.partial(kernel, (lax.axis_size("row"), lax.axis_size("col"))),
        out_shape=jax.ShapeDtypeStruct((4 * slots, 4 * slots), jnp.float32),
        in_specs=[any_space, any_space] + [pl.BlockSpec(memory_space=pltpu.SMEM)] * 2,
        out_specs=pl.BlockSpec(memory_space=pltpu.VMEM),
        scratch_shapes=[
            pltpu.VMEM((4, 9, points, points), jnp.float32),
            pltpu.VMEM((4, slots, slots), jnp.float32),
            pltpu.VMEM((4, 9, slots, points), jnp.float32),
            pltpu.VMEM((4, slots, 3 * points), jnp.bfloat16),
            pltpu.VMEM((2, 9, 4 * slots, points), jnp.bfloat16),
            pltpu.VMEM((COUNT, slots, points), jnp.float32),
            pltpu.VMEM((len(PACKED), small_rows, points // 2), jnp.float32),
            pltpu.VMEM((len(PACKED), small_rows, points // 2), jnp.float32),
            pltpu.VMEM((4, 9, 4 * slots, points), jnp.bfloat16),
            pltpu.VMEM((12, slots, points), jnp.float32),
            pltpu.VMEM((slots, strip_width), jnp.float32),
            pltpu.VMEM((slots, strip_width), jnp.float32),
            pltpu.VMEM((slots, strip_width), jnp.float32),
            pltpu.VMEM((slots, strip_width), jnp.float32),
            pltpu.SemaphoreType.DMA((COUNT,)),
            pltpu.SemaphoreType.DMA((COUNT,)),
            pltpu.SemaphoreType.DMA((20,)),
            pltpu.SemaphoreType.DMA((2 * len(STRIPS),)),
            pltpu.SemaphoreType.DMA((2 * len(STRIPS),)),
        ],
        compiler_params=pltpu.CompilerParams(
            vmem_limit_bytes=60 * 2**20, collective_id=0, has_side_effects=True
        ),
        name="skeletonize",
    )(boxes, interp, red_count, owner_flip)
    return parent[None, None]


def solution(mesh):
    in_specs = (
        P("row", "col", None, None, None, None),
        P("row", "col", None, None),
        P("row", "col"),
        P("row", "col", None),
    )
    out_specs = P("row", "col", None, None)
    return jax.shard_map(local, mesh=mesh, in_specs=in_specs, out_specs=out_specs, check_vma=False)
```

```python
import functools

import jax
import jax.numpy as jnp
from jax import lax
from jax.experimental import pallas as pl
from jax.experimental.pallas import tpu as pltpu
from jax.sharding import PartitionSpec as P

EXACT = lax.Precision.HIGHEST
GROUP = 8
BLOCK = 32
MESH = pl.DeviceIdType.MESH

FULL = [(a, e) for a in (-1, 0, 1) for e in (-1, 0, 1)]
TRAVEL = {
    "l0": [(0, -1), (1, 0), (-1, 0), (-1, -1), (1, -1), (0, 0)],
    "u0": [(-1, 0), (-1, -1), (0, -1), (0, 0), (-1, 1), (0, 1)],
    "d0": [(0, -1), (-1, 0), (-1, -1), (0, 0)],
    "r1": [(1, 1), (-1, 1), (-1, 0), (1, 0), (0, 1), (0, 0)],
    "u1": [(-1, -1), (-1, 0), (-1, 1), (0, -1), (0, 0), (0, 1)],
    "d1": [(-1, 1), (-1, 0), (0, 1), (0, 0)],
    "l2": [(0, -1), (0, 0), (-1, 0), (1, 0), (-1, -1), (1, -1)],
    "v2": [(1, 0), (1, 1)],
    "d2": [(1, -1)],
    "r3": [(-1, 1), (0, 1), (1, 1)],
    "v3": [(1, -1), (1, 0)],
    "d3": [(1, 1)],
}
FIRST = {}
COUNT = 0
for _name, _panels in TRAVEL.items():
    FIRST[_name] = COUNT
    COUNT += len(_panels)


STRIPS = {
    "A3": [(3, 0), (3, 1), (3, 2), (3, 3)],
    "A2": [(2, 0), (2, 1), (2, 2), (0, 0)],
    "A1": [(1, 0), (1, 1)],
    "E3": [(0, 3), (1, 3), (2, 3), (0, 1)],
    "E2": [(0, 2), (1, 2)],
}


def strip_places(slots):
    places, total = {}, 0
    for name, blocks in STRIPS.items():
        width = -(-len(blocks) * slots // 128) * 128
        places[name] = (total, width)
        total += width
    return places, total


PACKED = {("l0", (0, 0)), ("r1", (0, 1)), ("r1", (0, 0)), ("d0", (0, 0)), ("d1", (0, 1)), ("d1", (0, 0))}
PACKED |= {(name, k) for name in ("l2", "r3", "d2", "d3") for k in TRAVEL[name]} - {("l2", (0, -1))}
PACKED |= {("u0", (0, 0)), ("u1", (0, -1)), ("u1", (0, 0)), ("u1", (0, 1))}
PACKED = sorted(PACKED)


def slot(name, k):
    return FIRST[name] + TRAVEL[name].index(k)


def near_at(k):
    return (k[0] + 1) * 3 + k[1] + 1


def split(value):
    high = value.astype(jnp.bfloat16)
    low = (value - high.astype(jnp.float32)).astype(jnp.bfloat16)
    return high, low


def dot(left, right):
    return jnp.dot(left, right, preferred_element_type=jnp.float32)


def diagonal_inverse(block):
    size = block.shape[0]
    rows = lax.broadcasted_iota(jnp.int32, (size, size), 0)
    cols = lax.broadcasted_iota(jnp.int32, (size, size), 1)
    eye = (rows == cols).astype(jnp.float32)
    wide = jnp.concatenate([block, eye, jnp.zeros((size, 128 - 2 * size), jnp.float32)], axis=1)
    row_ids = lax.broadcasted_iota(jnp.int32, (size, 128), 0)
    scale = jnp.ones((size, 128), jnp.float32)
    for start in range(0, size, GROUP):
        columns = [
            jnp.broadcast_to(wide[:, start + q : start + q + 1], (size, 128)) for q in range(GROUP)
        ]
        for q in range(GROUP):
            at = start + q
            pivot = columns[q][at : at + 1, :]
            inverse = 1.0 / pivot
            below = jnp.where(row_ids > at, columns[q], 0.0)
            scale = jnp.where(row_ids == at, lax.rsqrt(pivot), scale)
            wide = wide - below * (wide[at : at + 1, :] * inverse)
            for p in range(q + 1, GROUP):
                columns[p] = columns[p] - below * (columns[p][at : at + 1, :] * inverse)
    return (wide * scale)[:, size : 2 * size]


def factor_inverse(matrix, hooks=()):
    size = matrix.shape[0]
    rows = lax.broadcasted_iota(jnp.int32, (size, size), 0)
    cols = lax.broadcasted_iota(jnp.int32, (size, size), 1)
    rest = matrix
    right = (rows == cols).astype(jnp.float32)
    done = []
    for start in range(0, size, BLOCK):
        inverse = diagonal_inverse(rest[:BLOCK, :BLOCK])
        top_right = jnp.dot(inverse, right[:BLOCK], precision=EXACT)
        done.append(top_right)
        if start + BLOCK < size:
            top = jnp.dot(inverse, rest[:BLOCK, BLOCK:], precision=EXACT)
            top_t = top.T
            rest = rest[BLOCK:, BLOCK:] - jnp.dot(top_t, top, precision=EXACT)
            right = right[BLOCK:] - jnp.dot(top_t, top_right, precision=EXACT)
        for at, hook in hooks:
            if at == start // BLOCK:
                hook()
    return jnp.concatenate(done, axis=0)


def kernel(sizes, near, interp_all, counts, flip, out, store, interp, panels, tops, stacks, arrived,
           packed, small, shared, pulled, own, first_got, chosen, last_got, send_sem, recv_sem, load_sem, strip_send,
           strip_recv):
    n_row, n_col = sizes
    points, slots = store.shape[-1], interp.shape[-1]
    low = points - slots
    row, col = lax.axis_index("row"), lax.axis_index("col")
    has = {
        "up": row > 0, "down": row < n_row - 1, "left": col > 0, "right": col < n_col - 1,
    }
    where_to = {
        "up": {"row": row - 1, "col": col}, "down": {"row": row + 1, "col": col},
        "left": {"row": row, "col": col - 1}, "right": {"row": row, "col": col + 1},
    }
    row_partner = {"row": row + 1 - 2 * lax.rem(row, 2), "col": col}
    col_partner = {"row": row, "col": col + 1 - 2 * lax.rem(col, 2)}

    loads = [pltpu.make_async_copy(near.at[i], store.at[i], load_sem.at[i]) for i in range(4)]
    loads += [
        pltpu.make_async_copy(interp_all.at[i // 2, i % 2], interp.at[i], load_sem.at[4 + i])
        for i in range(4)
    ]
    pulls = {}
    for y in range(4):
        for x in range(y):
            for one, two in ((x, y), (y, x)):
                k = near_at((two // 2 - one // 2, two % 2 - one % 2))
                n = len(pulls)
                pulls[one, two] = n, pltpu.make_async_copy(
                    near.at[one, k, pl.ds(low, slots), :], pulled.at[n], load_sem.at[8 + n]
                )
    for _, copy in pulls.values():
        copy.start()
    for i in (0, 4, 1, 5, 2, 6, 3, 7):
        loads[i].start()

    barrier = pltpu.get_barrier_semaphore()
    for way in has:
        @pl.when(has[way])
        def _(way=way):
            pl.semaphore_signal(barrier, inc=1, device_id=where_to[way], device_id_type=MESH)

    sent = []

    lanes = points // 2
    tail = points - low - lanes
    piece = slots * tail // lanes

    def pack(value, ref):
        ref[0:slots] = value[:, lanes:]
        lane_ids = lax.broadcasted_iota(jnp.int32, (piece, lanes), 1)
        folded = jnp.zeros((piece, lanes), jnp.float32)
        for i in range(slots // piece):
            part = pltpu.roll(value[i * piece : (i + 1) * piece, :lanes], (i * tail - low) % lanes, 1)
            inside = (lane_ids >= i * tail) & (lane_ids < (i + 1) * tail)
            folded = jnp.where(inside, part, folded)
        ref[slots:] = folded

    def unpack(ref):
        parts = [pltpu.roll(ref[slots:], (low - i * tail) % lanes, 1) for i in range(slots // piece)]
        front = jnp.concatenate(parts, axis=0)
        lane_ids = lax.broadcasted_iota(jnp.int32, (slots, lanes), 1)
        return jnp.concatenate([jnp.where(lane_ids >= low, front, 0.0), ref[0:slots]], axis=1)

    def landing(name, k):
        if (name, k) in PACKED:
            return small.at[PACKED.index((name, k))]
        return arrived.at[slot(name, k)]

    def copy_of(name, k, source, way):
        i = slot(name, k)
        return pltpu.make_async_remote_copy(
            src_ref=source, dst_ref=landing(name, k), send_sem=send_sem.at[i],
            recv_sem=recv_sem.at[i], device_id=where_to[way], device_id_type=MESH,
        )

    def send(name, k, source, way, and_also=None):
        if source is None:
            source = panels.at[int(name[1]), near_at(k)]
            if (name, k) in PACKED:
                staged = packed.at[PACKED.index((name, k))]
                pl.when(has[way])(lambda: pack(source[...], staged))
                source = staged
        copy = copy_of(name, k, source, way)
        sent.append((copy, way, and_also))
        if and_also is None:
            pl.when(has[way])(copy.start)
        else:
            pl.when(has[way] & has[and_also])(copy.start)

    def make_stack(value, ref):
        high, less = split(value)
        ref[0:slots] = high
        ref[slots : 2 * slots] = high
        ref[2 * slots : 3 * slots] = less
        ref[3 * slots : 4 * slots] = high

    def arrive(name, k):
        i = slot(name, k)
        pltpu.make_async_remote_copy(
            src_ref=landing(name, k), dst_ref=landing(name, k), send_sem=send_sem.at[i],
            recv_sem=recv_sem.at[i], device_id=where_to["up"], device_id_type=MESH,
        ).wait_recv()
        return unpack(landing(name, k)) if (name, k) in PACKED else arrived[i]

    def receive(name, k, stack):
        make_stack(arrive(name, k), stack.at[near_at(k)])

    def product(stack, one, two):
        return lax.dot_general(
            stack[near_at(one), 0 : 3 * slots], stack[near_at(two), slots : 4 * slots],
            (((0,), (0,)), ((), ())), preferred_element_type=jnp.float32,
        )

    def update(x, stack, one, twos):
        for two in twos:
            at = near_at((two[0] - one[0], two[1] - one[1]))
            store[x, at] = store[x, at] - product(stack, one, two)

    def update_rect(x, stack, one, rows, cols):
        base = near_at(one)

        def body(i, carry):
            a = rows[0] + i
            for e in cols:
                two = (a + 1) * 3 + e + 1
                at = (a - one[0] + 1) * 3 + e - one[1] + 1
                store[x, at] = store[x, at] - lax.dot_general(
                    stack[base, 0 : 3 * slots], stack[two, slots : 4 * slots],
                    (((0,), (0,)), ((), ())), preferred_element_type=jnp.float32,
                )
            return carry

        lax.fori_loop(0, len(rows), body, 0)

    def update_parent(x, stack, one, two):
        at = near_at((two[0] - one[0], two[1] - one[1]))
        store[x, at, low:] = store[x, at, low:] - product(stack, one, two)[low:]

    def panel_maker(x, hooks=()):
        red = counts[x // 2, x % 2]
        row_ids = lax.broadcasted_iota(jnp.int32, (slots, slots), 0)
        col_ids = lax.broadcasted_iota(jnp.int32, (slots, slots), 1)
        masked = jnp.where((row_ids < red) & (col_ids + low >= red), interp[x], 0.0)
        wide_rows = lax.broadcasted_iota(jnp.int32, (slots, points), 0)
        wide_cols = lax.broadcasted_iota(jnp.int32, (slots, points), 1)
        reduce = (wide_rows == wide_cols).astype(jnp.float32) - jnp.concatenate(
            [jnp.zeros((slots, low), jnp.float32), masked], axis=1
        )
        reduced = jnp.dot(reduce, store[x, 4], precision=EXACT)
        block = lax.dot_general(reduced, reduce, (((1,), (1,)), ((), ())), precision=EXACT)
        block = jnp.where(
            (row_ids < red) & (col_ids < red), block, (row_ids == col_ids).astype(jnp.float32)
        )
        block = 0.5 * (block + block.T)
        inverse = factor_inverse(block, hooks)
        inverse = jnp.where(col_ids < red, inverse, 0.0)
        whole_high, whole_low = split(jnp.dot(inverse, reduce, precision=EXACT))
        tops[x] = jnp.concatenate([whole_high, whole_high, whole_low], axis=1)

        def make(k):
            at = near_at(k)
            high, less = split(store[x, at])
            value = dot(tops[x], jnp.concatenate([high, less, high], axis=0))
            if k == (0, 0):
                value = jnp.where(wide_cols >= red, value, 0.0)
            panels[x, at] = value
            make_stack(value, stacks.at[x % 2, at])

        return make

    def keep(x, y):
        row_ids = lax.broadcasted_iota(jnp.int32, (slots, slots), 0) + low
        col_ids = lax.broadcasted_iota(jnp.int32, (slots, slots), 1) + low
        return (row_ids >= counts[x // 2, x % 2]) & (col_ids >= counts[y // 2, y % 2])

    places, _ = strip_places(slots)
    strip_at = list(STRIPS)

    def strip_copy(name, first_hop):
        along_row = first_hop == (name[0] == "A")
        i = strip_at.index(name) + (0 if first_hop else len(strip_at))
        first, width = places[name]
        source, target = (own, first_got) if first_hop else (chosen, last_got)
        return pltpu.make_async_remote_copy(
            src_ref=source.at[:, pl.ds(first, width)], dst_ref=target.at[:, pl.ds(first, width)],
            send_sem=strip_send.at[i], recv_sem=strip_recv.at[i],
            device_id=row_partner if along_row else col_partner, device_id_type=MESH,
        )

    def pick(name, first_hop):
        first, width = places[name]
        view = (slice(None), slice(first, first + width))
        axis = 0 if first_hop == (name[0] == "A") else 1
        flipped = jnp.full((slots, width), flip[0, 0, axis], jnp.int32) == 1
        if first_hop:
            return jnp.where(flipped, first_got[view], own[view])
        return jnp.where(flipped, last_got[view], chosen[view])

    def start_strip(name):
        for at, (x, y) in enumerate(STRIPS[name]):
            first = places[name][0] + at * slots
            at = near_at((y // 2 - x // 2, y % 2 - x % 2))
            if name[0] == "A":
                block = store[x, at, low:][:, low:]
            else:
                block = pulled[pulls[x, y][0]][:, low:] - pulled[pulls[y, x][0]][:, low:].T
            own[:, first : first + slots] = jnp.where(keep(x, y), block, 0.0)
        end = places[name][0] + len(STRIPS[name]) * slots
        if end < sum(places[name]):
            own[:, end : sum(places[name])] = jnp.zeros((slots, sum(places[name]) - end), jnp.float32)
        strip_copy(name, True).start()

    def pass_strip(name):
        strip_copy(name, True).wait_recv()
        first, width = places[name]
        chosen[:, first : first + width] = pick(name, True)
        strip_copy(name, False).start()

    def end_strip(name):
        strip_copy(name, False).wait_recv()
        value = pick(name, False)
        for at, (x, y) in enumerate(STRIPS[name]):
            block = value[:, at * slots : (at + 1) * slots]
            rows, cols = slice(x * slots, (x + 1) * slots), slice(y * slots, (y + 1) * slots)
            out[rows, cols] = block
            if name[0] == "A" and y < x:
                out[cols, rows] = out[cols, rows] + block.T

    def wait_load(i):
        loads[i].wait()
        loads[4 + i].wait()

    mine = [stacks.at[0], stacks.at[1], stacks.at[0], stacks.at[1]]
    from_right, from_down, from_left, other = (shared.at[i] for i in range(4))

    for _, copy in pulls.values():
        copy.wait()
    pl.semaphore_wait(barrier, sum(has[way].astype(jnp.int32) for way in has))
    start_strip("E3")
    wait_load(0)
    make = panel_maker(0)
    for k in TRAVEL["l0"] + [(-1, 1), (0, 1), (1, 1)]:
        make(k)
        if k in TRAVEL["l0"]:
            send("l0", k, None, "left")
        if k in TRAVEL["u0"]:
            send("u0", k, None, "up")
    wait_load(1)
    wait_load(2)
    wait_load(3)
    update_rect(1, mine[0], (0, 1), (-1, 0, 1), (0, 1))
    update_rect(2, mine[0], (1, 0), (0, 1), (-1, 0, 1))
    update_rect(3, mine[0], (1, 1), (0, 1), (0, 1))
    update_parent(0, mine[0], (0, 0), (0, 0))

    @pl.when(has["right"])
    def _():
        receive("l0", (0, -1), from_right)
        update(1, from_right, (0, -1), [(0, -1)])

    make_one = panel_maker(1)

    def finish_one(k):
        make_one(k)
        if k in TRAVEL["r1"]:
            send("r1", k, None, "right")
        if k in TRAVEL["u1"]:
            send("u1", k, None, "up")

    def step_one(k):
        @pl.when(has["right"])
        def _():
            receive("l0", k, from_right)
            update(1, from_right, (0, -1), [k])

        if k in TRAVEL["d0"][2:]:
            send("d0", k, landing("l0", k), "up", "right")
        finish_one((k[0], k[1] + 1))

    step_one((1, 0))
    step_one((-1, 0))
    finish_one((-1, -1))
    finish_one((1, -1))
    finish_one((0, -1))
    update(2, mine[1], (1, -1), [(1, -1), (0, -1)])
    update_parent(0, mine[1], (0, -1), (0, -1))

    @pl.when(has["down"])
    def _():
        for k in TRAVEL["u0"]:
            receive("u0", k, from_down)
        update_rect(2, from_down, (-1, 0), (-1, 0), (-1, 0, 1))
        update_rect(3, from_down, (-1, 1), (-1, 0), (0, 1))
        receive("u1", (-1, -1), from_down)
        update(2, from_down, (-1, -1), [(-1, -1)])

    @pl.when(has["left"])
    def _():
        receive("r1", (1, 1), from_left)
        update(2, from_left, (1, 1), [(1, 1)])
        arrive("r1", (-1, 1))

    send("d1", (-1, 1), landing("r1", (-1, 1)), "up", "left")
    for k in TRAVEL["d0"][:2]:
        send("d0", k, landing("l0", k), "up", "right")
    start_strip("E2")

    @pl.when(has["down"] & has["left"])
    def _():
        receive("d1", (-1, 1), other)
        update(2, other, (-1, 1), [(-1, 1)])

    def pass_on(k):
        pl.when(has["left"])(lambda: receive("r1", k, from_left))
        send("d1", k, landing("r1", k), "up", "left")

    def last_one():
        step_one((0, 0))
        finish_one((0, 0))

    make_two = panel_maker(2, [
        (0, lambda: step_one((-1, -1))), (1, lambda: step_one((1, -1))), (2, last_one),
        (3, lambda: pass_on((-1, 0))),
    ])

    @pl.when(has["left"])
    def _():
        receive("r1", (1, 0), from_left)
        update(2, from_left, (1, 1), [(1, 0)])

    @pl.when(has["down"] & has["left"])
    def _():
        receive("d1", (-1, 0), other)
        update(2, other, (-1, 1), [(-1, 0)])

    def finish_two(k):
        make_two(k)
        if k in TRAVEL["l2"]:
            send("l2", k, None, "left")
        if k in TRAVEL["v2"]:
            send("v2", k, None, "down")

    finish_two((0, -1))
    finish_two((0, 0))
    pass_on((0, 1))

    @pl.when(has["left"])
    def _():
        update(2, from_left, (1, 1), [(0, 1)])

    finish_two((-1, 0))

    @pl.when(has["down"])
    def _():
        for k in TRAVEL["u1"][1:]:
            receive("u1", k, from_down)
        update(2, from_down, (-1, -1), [(-1, 0), (0, -1), (0, 0)])

    update(2, mine[1], (1, -1), [(1, 0), (0, 0)])
    pass_on((0, 0))

    @pl.when(has["down"] & has["left"])
    def _():
        receive("d1", (0, 1), other)
        update(2, other, (-1, 1), [(0, 1)])

    finish_two((1, 0))

    @pl.when(has["left"])
    def _():
        update(2, from_left, (1, 1), [(0, 0)])
        update_parent(0, from_left, (0, 1), (0, 1))

    finish_two((-1, -1))

    @pl.when(has["down"] & has["left"])
    def _():
        receive("d1", (0, 0), other)
        update(2, other, (-1, 1), [(0, 0)])

    finish_two((1, -1))
    finish_two((1, 1))
    finish_two((0, 1))
    finish_two((-1, 1))
    update_rect(3, mine[2], (0, 1), (-1, 0, 1), (0, 1))
    update_rect(3, mine[1], (1, 0), (0, 1), (-1, 0, 1))
    update_parent(1, mine[1], (0, 0), (0, -1))
    update_parent(1, mine[1], (0, 0), (0, 0))

    @pl.when(has["right"])
    def _():
        update_rect(3, from_right, (1, -1), (0, 1), (-1, 0))

    @pl.when(has["down"])
    def _():
        update_rect(3, from_down, (-1, 0), (-1, 0), (-1, 0, 1))

    @pl.when(has["down"] & has["right"])
    def _():
        for k in TRAVEL["d0"]:
            receive("d0", k, other)
        update_rect(3, other, (-1, -1), (-1, 0), (-1, 0))

    @pl.when(has["right"])
    def _():
        receive("l2", (0, -1), from_right)
        update(3, from_right, (0, -1), [(0, -1)])

    make_three = panel_maker(3)
    pass_strip("E3")
    update_parent(0, mine[2], (-1, 0), (-1, 0))
    update_parent(1, mine[2], (-1, 1), (-1, 0))
    update_parent(1, mine[2], (-1, 1), (-1, 1))
    update_parent(2, mine[2], (0, 0), (-1, 0))
    update_parent(2, mine[2], (0, 0), (-1, 1))
    update_parent(2, mine[2], (0, 0), (0, 0))
    end_strip("E3")

    def finish_three(k):
        make_three(k)
        if k in TRAVEL["r3"]:
            send("r3", k, None, "right")
        if k in TRAVEL["v3"]:
            send("v3", k, None, "down")

    for k in TRAVEL["l2"][1:]:
        @pl.when(has["right"])
        def _(k=k):
            receive("l2", k, from_right)
            update(3, from_right, (0, -1), [k])

        if k in TRAVEL["d2"]:
            send("d2", k, landing("l2", k), "down", "right")
        finish_three((k[0], k[1] + 1))
    for k in ((1, -1), (0, 0), (-1, -1), (0, -1)):
        finish_three(k)

    corners = [(-1, -1), (-1, 0), (0, -1), (0, 0)]
    for y in range(4):
        update_parent(3, mine[3], corners[3], corners[y])
    start_strip("A3")
    pass_strip("E2")
    for x in range(3):
        for y in range(x + 1):
            update_parent(x, mine[3], corners[x], corners[y])
    pass_strip("A3")

    @pl.when(has["right"])
    def _():
        update_parent(1, from_right, (-1, -1), (-1, -1))

    @pl.when(has["up"])
    def _():
        receive("v2", (1, 0), from_down)
        receive("v2", (1, 1), from_down)
        update_parent(0, from_down, (1, 0), (1, 0))
        update_parent(1, from_down, (1, 1), (1, 0))
        update_parent(1, from_down, (1, 1), (1, 1))
        receive("v3", (1, -1), from_down)
        receive("v3", (1, 0), from_down)
        update_parent(0, from_down, (1, -1), (1, -1))
        update_parent(1, from_down, (1, 0), (1, -1))
        update_parent(1, from_down, (1, 0), (1, 0))

    @pl.when(has["up"] & has["right"])
    def _():
        receive("d2", (1, -1), other)
        update_parent(1, other, (1, -1), (1, -1))

    start_strip("A1")

    @pl.when(has["left"])
    def _():
        for k in TRAVEL["r3"]:
            receive("r3", k, from_left)

    send("d3", (1, 1), landing("r3", (1, 1)), "down", "left")

    @pl.when(has["left"])
    def _():
        update_parent(0, from_left, (-1, 1), (-1, 1))
        update_parent(2, from_left, (0, 1), (-1, 1))
        update_parent(2, from_left, (0, 1), (0, 1))

    pass_strip("A1")

    @pl.when(has["up"] & has["left"])
    def _():
        receive("d3", (1, 1), other)
        update_parent(0, other, (1, 1), (1, 1))

    start_strip("A2")
    pass_strip("A2")
    for name in ("E2", "A3", "A1", "A2"):
        end_strip(name)
    for copy, way, and_also in sent:
        if and_also is None:
            pl.when(has[way])(copy.wait_send)
        else:
            pl.when(has[way] & has[and_also])(copy.wait_send)
    for name in STRIPS:
        strip_copy(name, True).wait_send()
        strip_copy(name, False).wait_send()


def local(near, interp, red_count, owner_flip):
    points, slots = near.shape[-1], interp.shape[-1]
    boxes = near.reshape(4, 9, points, points)
    strip_width = strip_places(slots)[1]
    small_rows = 2 * slots * slots // points
    any_space = pl.BlockSpec(memory_space=pl.ANY)
    parent = pl.pallas_call(
        functools.partial(kernel, (lax.axis_size("row"), lax.axis_size("col"))),
        out_shape=jax.ShapeDtypeStruct((4 * slots, 4 * slots), jnp.float32),
        in_specs=[any_space, any_space] + [pl.BlockSpec(memory_space=pltpu.SMEM)] * 2,
        out_specs=pl.BlockSpec(memory_space=pltpu.VMEM),
        scratch_shapes=[
            pltpu.VMEM((4, 9, points, points), jnp.float32),
            pltpu.VMEM((4, slots, slots), jnp.float32),
            pltpu.VMEM((4, 9, slots, points), jnp.float32),
            pltpu.VMEM((4, slots, 3 * points), jnp.bfloat16),
            pltpu.VMEM((2, 9, 4 * slots, points), jnp.bfloat16),
            pltpu.VMEM((COUNT, slots, points), jnp.float32),
            pltpu.VMEM((len(PACKED), small_rows, points // 2), jnp.float32),
            pltpu.VMEM((len(PACKED), small_rows, points // 2), jnp.float32),
            pltpu.VMEM((4, 9, 4 * slots, points), jnp.bfloat16),
            pltpu.VMEM((12, slots, points), jnp.float32),
            pltpu.VMEM((slots, strip_width), jnp.float32),
            pltpu.VMEM((slots, strip_width), jnp.float32),
            pltpu.VMEM((slots, strip_width), jnp.float32),
            pltpu.VMEM((slots, strip_width), jnp.float32),
            pltpu.SemaphoreType.DMA((COUNT,)),
            pltpu.SemaphoreType.DMA((COUNT,)),
            pltpu.SemaphoreType.DMA((20,)),
            pltpu.SemaphoreType.DMA((2 * len(STRIPS),)),
            pltpu.SemaphoreType.DMA((2 * len(STRIPS),)),
        ],
        compiler_params=pltpu.CompilerParams(
            vmem_limit_bytes=60 * 2**20, collective_id=0, has_side_effects=True
        ),
        name="skeletonize",
    )(boxes, interp, red_count, owner_flip)
    return parent[None, None]


def solution(mesh):
    in_specs = (
        P("row", "col", None, None, None, None),
        P("row", "col", None, None),
        P("row", "col"),
        P("row", "col", None),
    )
    out_specs = P("row", "col", None, None)
    return jax.shard_map(local, mesh=mesh, in_specs=in_specs, out_specs=out_specs, check_vma=False)
```
